32 devices in a mesh: group: 4 (over y, core), inner: 8 (over z, x).
Axes of the slice: x: 2, y: 2, z: 4, core: 2. Of those that a mesh axis runs over, the one named last changes fastest.
Arguments:
- grad_out: bfloat16 [4096, 2048], P(('group', 'inner')), may hold values from -4 to 4
- hidden_in: bfloat16 [4096, 2048], P(('group', 'inner')), may hold values from -6 to 6
- norm_gain: float32 [2048], replicated, may hold values from 0.5 to 1.5
- expert_ids: int32 [4096, 8], P(('group', 'inner')), may hold values from 0 to 31, all different within a row; in each aligned block of 128 rows (0 to 127, 128 to 255, ...) at most 40 rows name the same one
- gate_weights: float32 [4096, 8], P(('group', 'inner')), may hold values from 0.02 to 0.5
- gate_proj: bfloat16 [32, 2048, 768], P(('group', 'inner')), may hold values from -0.125 to 0.125
- up_proj: bfloat16 [32, 2048, 768], P(('group', 'inner')), may hold values from -0.125 to 0.125
- down_proj: bfloat16 [32, 768, 2048], P(('group', 'inner')), may hold values from -0.21875 to 0.21875
- out_proj: bfloat16 [4096, 2048], P('inner'), may hold values from -0.09375 to 0.09375
- query_rows: bfloat16 [4096, 4096], P('group', 'inner'), may hold values from -140 to 140
- key_rows: bfloat16 [4096, 4096], P('group', 'inner'), may hold values from -7 to 7
- value_rows: bfloat16 [4096, 4096], P('group', 'inner'), may hold values from -6 to 6
Outputs:
- grad_hidden: bfloat16 [4096, 2048], P(('group', 'inner'))
- grad_gate: bfloat16 [4096, 8], P(('group', 'inner'))
- grad_queries: bfloat16 [4096, 4096], P('group', 'inner')
- grad_keys: bfloat16 [4096, 4096], P('group', 'inner')
- grad_values: bfloat16 [4096, 4096], P('group', 'inner')
The draws below stay inside these ranges and needn't reach their ends.
Inputs may be any that keep to these rules, and one draw needn't show every extreme that they name: `expert_ids`: each row names 8 different experts; in the rows of one device no expert is named more than 40 times, a bound that some block reaches.
All inputs are finite; a program needn't handle non-finite values.
Results may differ from the reference program's by a relative error of at most 0.019.
Values may be sent and summed in bfloat16 or wider, within the bound.
A program may use at most 128 MiB of HBM per device.

```python
import math
import jax
import jax.numpy as jnp
import numpy as np
from jax import lax

D = 2048
FF = 768
HEADS = 32
HD = 128
TOP = 8
TOK_DEV = 128
EXPERTS = 32
CAP = 40
TOKENS = 4096
LEN = 512
N_GROUP = 4
N_INNER = 8


def joint_draw(key):
    base = jax.random.fold_in(key, 7123)
    first, second = jax.random.split(base, 2)
    shape = (TOKENS, HEADS, HD)
    key_vals = jax.random.truncated_normal(first, -6.0, 6.0, shape, jnp.float32)
    query_vals = jax.random.truncated_normal(second, -6.0, 6.0, shape, jnp.float32)
    return (query_vals.reshape(TOKENS, HEADS * HD), key_vals.reshape(TOKENS, HEADS * HD))


def draw_query_rows(key, part):
    return joint_draw(key)[0].astype(jnp.bfloat16)


def draw_key_rows(key, part):
    return joint_draw(key)[1].astype(jnp.bfloat16)


def block_levels(own_key, extent, shards, least, largest):
    gain = 1.0
    for dim, blocks in shards:
        steps = jax.random.uniform(jax.random.fold_in(jax.random.fold_in(own_key, 6), dim), (blocks,), jnp.float32, least / len(shards), largest / len(shards))
        gain = gain * jnp.repeat(jnp.exp(steps), extent[dim] // blocks).reshape((-1,) + (1,) * (len(extent) - 1 - dim))
    return gain


def deal_out(rng, own, number, rows, number_of, top, reach, lean):
    order = jax.random.permutation(rng, number_of)
    heavy_load, usual = portions_of(number_of, rows * top, reach, lean, True), portions_of(number_of, rows * top, reach, lean, False)
    places = jnp.arange(number_of)

    def named(lengths, offset_by):
        used = int((lengths > 0).sum())
        fixed = max(1, used // 4)
        shifted = fixed + (places - fixed + offset_by * (used - fixed)) % max(1, number_of - fixed)
        return jnp.zeros((number_of,), jnp.int32).at[order[jnp.where(places < fixed, places, shifted)]].set(jnp.asarray(lengths, jnp.int32))

    lengths = jnp.where(number % 4 == 0, named(heavy_load, number // 4), named(usual, number - number // 4 - 1))
    mixed = jax.random.permutation(jax.random.fold_in(own, 3), number_of)
    source_of, receiver = mixed[0:number_of // 2 * 2:2], mixed[1:number_of // 2 * 2:2]
    margin = jnp.minimum(lengths[source_of] - 1, reach - lengths[receiver]) // 2
    margin = jnp.where((source_of == order[0]) | (receiver == order[0]) | (lengths[receiver] == 0), 0, jnp.maximum(margin, 0))
    shifted = jax.random.randint(jax.random.fold_in(own, 4), (number_of // 2,), 0, 1 << 20) % (margin + 1)
    lengths = lengths.at[source_of].add(-shifted).at[receiver].add(shifted)
    members = jnp.searchsorted(jnp.cumsum(lengths), jnp.arange(rows * top), side="right").astype(jnp.int32)
    listing = members.reshape(top, rows).T
    listing = listing[jax.random.permutation(jax.random.fold_in(own, 1), rows)]
    offset_by = jax.random.randint(jax.random.fold_in(own, 2), (rows, 1), 0, top)
    return jnp.take_along_axis(listing, (jnp.arange(top)[None, :] + offset_by) % top, axis=1)


def portions_of(count, total, reach, skew, full):
    weights = [(1 << 20) // math.isqrt(standing ** skew) + 1 for standing in range(1, count + 1)]
    largest = reach if full else min(reach, max(-(-total // count), total * weights[0] // sum(weights)))
    least = 1 if total - largest >= count - 1 else 0
    holding, rest = [largest] + [least] * (count - 1), total - largest - least * (count - 1)
    while rest > 0:
        movable = [i for i in range(1, count) if holding[i] < largest] or [i for i in range(1, count) if holding[i] < reach]
        pool, remaining = sum([weights[i] for i in movable]), rest
        for i in movable:
            more = min(reach - holding[i], max(1, remaining * weights[i] // pool), rest)
            holding[i] = holding[i] + more
            rest = rest - more
    return np.array(holding)


def normal_values(rng, shape, deviation, reach, pieces=(), held_as=jnp.bfloat16):
    entries = jax.random.normal(rng, shape, jnp.float32) * deviation
    if len(pieces) > 0:
        entries = block_levels(rng, shape, pieces, -0.22, 0.18) * entries
    return jnp.clip(entries, min=-reach, max=reach).astype(held_as)


def setup_inputs(seed: int = 0) -> dict:
    key_list = jax.random.split(jax.random.key(seed), 13)
    grad_out = normal_values(key_list[0], (TOKENS, D), 0.5, 4.0, ((0, 32),))
    hidden_in = normal_values(key_list[1], (TOKENS, D), 1.0, 6.0, ((0, 32),))
    norm_gain = jnp.clip(1.0 + 0.1 * jax.random.normal(key_list[2], (D,), jnp.float32), 0.5, 1.5)
    expert_ids_keys = jax.random.split(jax.random.fold_in(key_list[3], 1), TOKENS // TOK_DEV)
    expert_ids_turns = jax.random.permutation(jax.random.fold_in(key_list[3], 3), TOKENS // TOK_DEV)
    expert_ids = jax.vmap(lambda own, number: deal_out(jax.random.fold_in(key_list[3], 2), own, number, TOK_DEV, EXPERTS, TOP, CAP, 2))(expert_ids_keys, expert_ids_turns).reshape((TOKENS, TOP))
    gate_weights = jnp.clip(jnp.exp(math.log(0.5) - 3.218876 * jax.random.uniform(key_list[4], (TOKENS, TOP), jnp.float32) ** block_levels(key_list[4], (TOKENS, TOP), ((0, 32),), -0.2, 0.2)), 0.02, 0.5)
    gate_proj = normal_values(key_list[5], (EXPERTS, D, FF), D ** -0.5, 0.125, ((0, 32),))
    up_proj = normal_values(key_list[6], (EXPERTS, D, FF), D ** -0.5, 0.125, ((0, 32),))
    down_proj = normal_values(key_list[7], (EXPERTS, FF, D), FF ** -0.5, 0.21875, ((0, 32),))
    out_proj = normal_values(key_list[8], (HEADS * HD, D), (HEADS * HD) ** -0.5, 0.09375, ((0, 8),))
    query_rows = draw_query_rows(jax.random.fold_in(key_list[12], 71), 0)
    key_rows = draw_key_rows(jax.random.fold_in(key_list[12], 71), 0)
    value_rows = normal_values(key_list[11], (TOKENS, HEADS * HD), 1.0, 6.0, ((0, 4), (1, 8)))
    return dict(grad_out=grad_out, hidden_in=hidden_in, norm_gain=norm_gain, expert_ids=expert_ids, gate_weights=gate_weights, gate_proj=gate_proj, up_proj=up_proj, down_proj=down_proj, out_proj=out_proj, query_rows=query_rows, key_rows=key_rows, value_rows=value_rows)


def dot_rt(left, right):
    return lax.dot_general(left, right, (((1,), (1,)), ((), ())), preferred_element_type=jnp.float32)

def expert_backward(grad_in, normed_in, gate_mat, up_mat, down_mat):
    gate_pre = jnp.dot(normed_in, gate_mat, preferred_element_type=jnp.float32)
    up_pre = jnp.dot(normed_in, up_mat, preferred_element_type=jnp.float32)
    sigma = jax.nn.sigmoid(gate_pre)
    act = gate_pre * sigma
    slope = sigma * (1.0 + gate_pre * (1.0 - sigma))
    expert_hidden = act * up_pre
    grad_hid = dot_rt(grad_in, down_mat)
    gate_score = lax.optimization_barrier(jnp.sum(grad_hid * expert_hidden, axis=1)).astype(jnp.bfloat16)
    grad_gatepre = (grad_hid * up_pre * slope).astype(jnp.bfloat16)
    grad_uppre = (grad_hid * act).astype(jnp.bfloat16)
    pair_grad = (dot_rt(grad_gatepre, gate_mat) + dot_rt(grad_uppre, up_mat)).astype(jnp.bfloat16)
    return (pair_grad, gate_score)

def attention_grads(grad_attn, query_rows, key_rows, value_rows):
    seq_count = query_rows.shape[0] // LEN

    def by_head(matrix):
        return matrix.reshape(seq_count, LEN, HEADS, HD).transpose(2, 0, 1, 3).astype(jnp.float32)
    att_scale = HD ** (-0.5)
    causal = jnp.arange(LEN)[:, None] >= jnp.arange(LEN)[None, :]

    def one_head(block_item):
        query, key_part, value, grad_part = block_item
        scores = jnp.einsum('sqd,skd->sqk', query, key_part) * att_scale
        scores = jnp.where(causal[None], scores, -jnp.inf)
        peak = lax.optimization_barrier(jnp.max(scores, axis=2, keepdims=True))
        exp_scores = jnp.exp(scores - peak)
        probs = exp_scores / lax.optimization_barrier(jnp.sum(exp_scores, axis=2, keepdims=True))
        probs_half = lax.optimization_barrier(probs.astype(jnp.bfloat16)).astype(jnp.float32)
        grad_v = jnp.einsum('sqk,sqd->skd', probs_half, grad_part).astype(jnp.bfloat16)
        grad_probs = jnp.einsum('sqd,skd->sqk', grad_part, value)
        delta = lax.optimization_barrier(jnp.sum(probs * grad_probs, axis=2, keepdims=True))
        grad_scores = lax.optimization_barrier((probs * (grad_probs - delta)).astype(jnp.bfloat16)).astype(jnp.float32)
        grad_q = (att_scale * jnp.einsum('sqk,skd->sqd', grad_scores, key_part)).astype(jnp.bfloat16)
        grad_k = (att_scale * jnp.einsum('sqk,sqd->skd', grad_scores, query)).astype(jnp.bfloat16)
        return (grad_q, grad_k, grad_v)
    stacked = lax.map(one_head, (by_head(query_rows), by_head(key_rows), by_head(value_rows), by_head(grad_attn)))

    def by_token(result):
        return result.transpose(1, 2, 0, 3).reshape(seq_count * LEN, HEADS * HD)
    return (by_token(stacked[0]), by_token(stacked[1]), by_token(stacked[2]))

def reference(grad_out, hidden_in, norm_gain, expert_ids, gate_weights, gate_proj, up_proj, down_proj, out_proj, query_rows, key_rows, value_rows):
    token_count, model_width = grad_out.shape
    hid_full = hidden_in.astype(jnp.float32)
    inv_rms = lax.rsqrt(lax.optimization_barrier(jnp.mean(hid_full * hid_full, axis=1, keepdims=True)) + 1e-06)
    normal_rows = hid_full * inv_rms
    normed = (normal_rows * norm_gain).astype(jnp.bfloat16)
    flat_ids = expert_ids.reshape(-1).astype(jnp.int32)
    pair_count = flat_ids.shape[0]
    flat_gates = gate_weights.reshape(-1)
    order = jnp.argsort(flat_ids, stable=True).astype(jnp.int32)
    counts = jnp.bincount(flat_ids, length=EXPERTS).astype(jnp.int32)
    starts = (jnp.cumsum(counts) - counts).astype(jnp.int32)
    bound = N_GROUP * N_INNER * CAP

    def per_expert(carry, expert):
        moe_grad, gate_grad = carry
        position = starts[expert] + jnp.arange(bound, dtype=jnp.int32)
        valid = jnp.arange(bound, dtype=jnp.int32) < counts[expert]
        pair_index = order[jnp.minimum(position, pair_count - 1)].astype(jnp.int32)
        token_index = (pair_index // TOP).astype(jnp.int32)
        pair_grad, gate_score = expert_backward(grad_out[token_index], normed[token_index], gate_proj[expert], up_proj[expert], down_proj[expert])
        weight = jnp.where(valid, flat_gates[pair_index], 0.0)
        pair_full = lax.optimization_barrier(pair_grad).astype(jnp.float32)
        moe_grad = moe_grad.at[token_index].add(weight[:, None] * pair_full)
        score_full = lax.optimization_barrier(gate_score).astype(jnp.float32)
        gate_grad = gate_grad.at[pair_index].add(jnp.where(valid, score_full, 0.0))
        return ((moe_grad, gate_grad), None)
    start_carry = (jnp.zeros((token_count, model_width), jnp.float32), jnp.zeros((pair_count,), jnp.float32))
    (moe_grad, gate_grad), unused = lax.scan(per_expert, start_carry, jnp.arange(EXPERTS, dtype=jnp.int32))
    grad_gate = gate_grad.reshape(token_count, TOP).astype(jnp.bfloat16)
    scaled = moe_grad * norm_gain
    inner_mean = lax.optimization_barrier(jnp.mean(scaled * normal_rows, axis=1, keepdims=True))
    grad_hidden = (grad_out.astype(jnp.float32) + inv_rms * (scaled - normal_rows * inner_mean)).astype(jnp.bfloat16)
    grad_attn = dot_rt(grad_hidden, out_proj).astype(jnp.bfloat16)
    grad_queries, grad_keys, grad_values = attention_grads(grad_attn, query_rows, key_rows, value_rows)
    return (grad_hidden, grad_gate, grad_queries, grad_keys, grad_values)
```

```python
import functools

import jax
import jax.numpy as jnp
from jax import lax
from jax.experimental import pallas as pl
from jax.experimental.pallas import tpu as pltpu
from jax.sharding import PartitionSpec as P

HD = 128
SEQS = 2
AXES = ("group", "inner")


def dot_rt(left, right):
    return lax.dot_general(
        left, right, (((1,), (1,)), ((), ())), preferred_element_type=jnp.float32
    )


def dot_lt(left, right):
    return lax.dot_general(
        left, right, (((0,), (0,)), ((), ())), preferred_element_type=jnp.float32
    )


def expert_backward(grad_in, normed_in, gate_mat, up_mat, down_mat):
    gate_pre = jnp.dot(normed_in, gate_mat, preferred_element_type=jnp.float32)
    up_pre = jnp.dot(normed_in, up_mat, preferred_element_type=jnp.float32)
    sigma = jax.nn.sigmoid(gate_pre)
    act = gate_pre * sigma
    slope = sigma * (1.0 + gate_pre * (1.0 - sigma))
    expert_hidden = act * up_pre
    grad_hid = dot_rt(grad_in, down_mat)
    gate_score = jnp.sum(grad_hid * expert_hidden, axis=1).astype(jnp.bfloat16)
    grad_gatepre = (grad_hid * up_pre * slope).astype(jnp.bfloat16)
    grad_uppre = (grad_hid * act).astype(jnp.bfloat16)
    pair_grad = (dot_rt(grad_gatepre, gate_mat) + dot_rt(grad_uppre, up_mat)).astype(jnp.bfloat16)
    return (pair_grad, gate_score)


def attention_kernel(rows_ref, proj_ref, q_ref, k_ref, v_ref, gq_ref, gk_ref, gv_ref):
    length = q_ref.shape[0]
    att_scale = HD ** (-0.5)
    block = 256 if length % 256 == 0 else length
    count = length // block
    grad_part = dot_rt(rows_ref[...], proj_ref[...]).astype(jnp.bfloat16)
    grad_k = [None] * count
    grad_v = [None] * count
    for i in range(count):
        lo, hi = i * block, (i + 1) * block
        query = q_ref[lo:hi, :]
        grad_i = grad_part[lo:hi, :]
        keys = k_ref[:hi, :]
        scores = dot_rt(query, keys) * att_scale
        rows = lax.broadcasted_iota(jnp.int32, (block, hi), 0) + lo
        cols = lax.broadcasted_iota(jnp.int32, (block, hi), 1)
        scores = jnp.where(rows >= cols, scores, -jnp.inf)
        peak = jnp.max(scores, axis=1, keepdims=True)
        exp_scores = jnp.exp(scores - peak)
        probs = exp_scores * (1.0 / jnp.sum(exp_scores, axis=1, keepdims=True))
        probs_half = probs.astype(jnp.bfloat16)
        grad_probs = dot_rt(grad_i, v_ref[:hi, :])
        delta = jnp.sum(probs * grad_probs, axis=1, keepdims=True)
        grad_scores = (probs * (grad_probs - delta)).astype(jnp.bfloat16)
        gq_ref[lo:hi, :] = (
            att_scale * jnp.dot(grad_scores, keys, preferred_element_type=jnp.float32)
        ).astype(jnp.bfloat16)
        part_v = dot_lt(probs_half, grad_i)
        part_k = dot_lt(grad_scores, query)
        for j in range(i + 1):
            piece_v = part_v[j * block : (j + 1) * block, :]
            piece_k = part_k[j * block : (j + 1) * block, :]
            grad_v[j] = piece_v if grad_v[j] is None else grad_v[j] + piece_v
            grad_k[j] = piece_k if grad_k[j] is None else grad_k[j] + piece_k
    for j in range(count):
        gk_ref[j * block : (j + 1) * block, :] = (att_scale * grad_k[j]).astype(jnp.bfloat16)
        gv_ref[j * block : (j + 1) * block, :] = grad_v[j].astype(jnp.bfloat16)


def attention_grads(rows, proj, query_rows, key_rows, value_rows):
    total, width = rows.shape
    length = total // SEQS
    heads = proj.shape[0] // HD
    tile = pl.BlockSpec((length, HD), lambda s, h: (s, h))
    out = jax.ShapeDtypeStruct(query_rows.shape, jnp.bfloat16)
    return pl.pallas_call(
        attention_kernel,
        grid=(SEQS, heads),
        in_specs=[
            pl.BlockSpec((length, width), lambda s, h: (s, 0)),
            pl.BlockSpec((HD, width), lambda s, h: (h, 0)),
            tile,
            tile,
            tile,
        ],
        out_specs=[tile, tile, tile],
        out_shape=[out, out, out],
        compiler_params=pltpu.CompilerParams(
            dimension_semantics=("arbitrary", "arbitrary"),
            vmem_limit_bytes=48 * 1024 * 1024,
        ),
    )(rows, proj, query_rows, key_rows, value_rows)


def local(
    grad_out,
    hidden_in,
    norm_gain,
    expert_ids,
    gate_weights,
    gate_proj,
    up_proj,
    down_proj,
    out_proj,
    query_rows,
    key_rows,
    value_rows,
):
    tok_dev, model_width = grad_out.shape
    top_count = expert_ids.shape[1]
    groups = lax.axis_size("group")
    inner_size = lax.axis_size("inner")
    experts = groups * inner_size
    capacity = max(2, 5 * tok_dev * top_count // (4 * experts))
    near = 2
    far = inner_size // near
    plane = groups * near
    my_group = lax.axis_index("group")
    my_inner = lax.axis_index("inner")
    my_far = my_inner // near
    my_spot = my_group * near + my_inner % near

    def along(shift):
        pairs = []
        for dev in range(experts):
            g, i = divmod(dev, inner_size)
            f, n = divmod(i, near)
            pairs.append((dev, g * inner_size + (f ^ shift) * near + n))
        return pairs

    def across(turn):
        pairs = []
        for dev in range(experts):
            g, i = divmod(dev, inner_size)
            f, n = divmod(i, near)
            g2, n2 = divmod((g * near + n) ^ turn, near)
            pairs.append((dev, g2 * inner_size + f * near + n2))
        return pairs

    hid_full = hidden_in.astype(jnp.float32)
    inv_rms = lax.rsqrt(jnp.mean(hid_full * hid_full, axis=1, keepdims=True) + 1e-06)
    normal_rows = hid_full * inv_rms
    normed = (normal_rows * norm_gain).astype(jnp.bfloat16)
    token_rows = jnp.concatenate([grad_out, normed], axis=1)

    spots = my_spot ^ jnp.arange(plane, dtype=jnp.int32)
    plane_experts = (spots // near) * inner_size + my_far * near + spots % near
    before = (
        jnp.arange(tok_dev)[:, None] > jnp.arange(tok_dev)[None, :]
    ).astype(jnp.bfloat16)
    slots = jnp.arange(capacity, dtype=jnp.float32)

    chunk_rows = [token_rows]
    chunk_ids = [expert_ids]
    chunk_gates = [gate_weights]
    for s in range(1, far):
        chunk_ids.append(lax.ppermute(expert_ids, AXES, along(s)))
        chunk_gates.append(lax.ppermute(gate_weights, AXES, along(s)))
        chunk_rows.append(lax.ppermute(token_rows, AXES, along(s)))

    total = None
    scores = []
    for s in range(far):
        ids, gates, rows = chunk_ids[s], chunk_gates[s], chunk_rows[s]
        hit = ids[:, :, None] == plane_experts[None, None, :]
        match = jnp.any(hit, axis=1)
        gate_of = jnp.sum(jnp.where(hit, gates[:, :, None], 0.0), axis=1)
        rank = jnp.dot(before, match.astype(jnp.bfloat16), preferred_element_type=jnp.float32)
        place = jnp.where(match, rank, -1.0)
        put = (place.T[:, None, :] == slots[None, :, None]).astype(jnp.bfloat16)
        packed = jnp.dot(
            put.reshape(plane * capacity, tok_dev), rows, preferred_element_type=jnp.float32
        ).astype(jnp.bfloat16)
        packed = packed.reshape(plane, capacity, 2 * model_width)
        arrived = [packed[0]]
        for d in range(1, plane):
            arrived.append(lax.ppermute(packed[d], AXES, across(d)))
        arrived = jnp.concatenate(arrived, axis=0)
        pair_grad, gate_score = expert_backward(
            arrived[:, :model_width],
            arrived[:, model_width:],
            gate_proj[0],
            up_proj[0],
            down_proj[0],
        )
        scores.append(gate_score.reshape(plane, capacity))
        pair_grad = pair_grad.reshape(plane, capacity, model_width)
        back = [pair_grad[0]]
        for d in range(1, plane):
            back.append(lax.ppermute(pair_grad[d], AXES, across(d)))
        back = jnp.concatenate(back, axis=0)
        weight = jnp.where(
            place[:, :, None] == slots[None, None, :], gate_of[:, :, None], 0.0
        ).reshape(tok_dev, plane * capacity)
        high = weight.astype(jnp.bfloat16)
        low = (weight - high.astype(jnp.float32)).astype(jnp.bfloat16)
        part = jnp.dot(high, back, preferred_element_type=jnp.float32) + jnp.dot(
            low, back, preferred_element_type=jnp.float32
        )
        if s > 0:
            part = lax.ppermute(part.astype(jnp.bfloat16), AXES, along(s)).astype(jnp.float32)
        total = part if total is None else total + part
    moe_grad = total

    score_all = jnp.stack(scores)
    far_order = my_far ^ jnp.arange(far, dtype=jnp.int32)
    spot_order = my_spot ^ jnp.arange(plane, dtype=jnp.int32)
    score_all = score_all[far_order][:, spot_order]
    score_send = (
        score_all.reshape(far, groups, near, capacity)
        .transpose(1, 0, 2, 3)
        .reshape(experts, capacity)
    )
    score_back = lax.all_to_all(score_send, AXES, split_axis=0, concat_axis=0, tiled=True)
    own_hit = expert_ids[:, :, None] == jnp.arange(experts, dtype=jnp.int32)[None, None, :]
    own_match = jnp.any(own_hit, axis=1)
    own_rank = jnp.dot(before, own_match.astype(jnp.bfloat16), preferred_element_type=jnp.float32)
    own_score = jnp.sum(
        jnp.where(
            own_rank[:, :, None] == slots[None, None, :],
            score_back.astype(jnp.float32)[None],
            0.0,
        ),
        axis=2,
    )
    grad_gate = jnp.sum(jnp.where(own_hit, own_score[:, None, :], 0.0), axis=2).astype(
        jnp.bfloat16
    )

    scaled = moe_grad * norm_gain
    inner_mean = jnp.mean(scaled * normal_rows, axis=1, keepdims=True)
    grad_hidden = (
        grad_out.astype(jnp.float32) + inv_rms * (scaled - normal_rows * inner_mean)
    ).astype(jnp.bfloat16)
    gathered = lax.all_gather(grad_hidden, "inner", axis=0, tiled=True)
    grad_q, grad_k, grad_v = attention_grads(gathered, out_proj, query_rows, key_rows, value_rows)
    return (grad_hidden, grad_gate, grad_q, grad_k, grad_v)


def solution(mesh):
    in_specs = (
        P(("group", "inner"), None),
        P(("group", "inner"), None),
        P(),
        P(("group", "inner"), None),
        P(("group", "inner"), None),
        P(("group", "inner"), None, None),
        P(("group", "inner"), None, None),
        P(("group", "inner"), None, None),
        P("inner", None),
        P("group", "inner"),
        P("group", "inner"),
        P("group", "inner"),
    )
    out_specs = (
        P(("group", "inner"), None),
        P(("group", "inner"), None),
        P("group", "inner"),
        P("group", "inner"),
        P("group", "inner"),
    )
    return jax.shard_map(local, mesh=mesh, in_specs=in_specs, out_specs=out_specs, check_vma=False)
```

```python
import jax
import jax.numpy as jnp
from jax import lax
from jax.experimental import pallas as pl
from jax.experimental.pallas import tpu as pltpu
from jax.sharding import PartitionSpec as P


HD = 128
SEQS = 2
AXES = ("group", "inner")


def dot_rt(left, right):
    return lax.dot_general(
        left, right, (((1,), (1,)), ((), ())), preferred_element_type=jnp.float32
    )


def dot_lt(left, right):
    return lax.dot_general(
        left, right, (((0,), (0,)), ((), ())), preferred_element_type=jnp.float32
    )


def expert_backward(grad_in, normed_in, gate_mat, up_mat, down_mat):
    gate_pre = jnp.dot(normed_in, gate_mat, preferred_element_type=jnp.float32)
    up_pre = jnp.dot(normed_in, up_mat, preferred_element_type=jnp.float32)
    sigma = jax.nn.sigmoid(gate_pre)
    act = gate_pre * sigma
    slope = sigma * (1.0 + gate_pre * (1.0 - sigma))
    expert_hidden = act * up_pre
    grad_hid = dot_rt(grad_in, down_mat)
    gate_score = jnp.sum(grad_hid * expert_hidden, axis=1).astype(jnp.bfloat16)
    grad_gatepre = (grad_hid * up_pre * slope).astype(jnp.bfloat16)
    grad_uppre = (grad_hid * act).astype(jnp.bfloat16)
    pair_grad = (dot_rt(grad_gatepre, gate_mat) + dot_rt(grad_uppre, up_mat)).astype(jnp.bfloat16)
    return (pair_grad, gate_score)


def row_block(length):
    return 256 if length % 256 == 0 else length


def probs_kernel(q_ref, k_ref, probs_ref):
    length = q_ref.shape[0]
    block = row_block(length)
    att_scale = HD ** (-0.5)
    for i in range(length // block):
        lo, hi = i * block, (i + 1) * block
        scores = dot_rt(q_ref[lo:hi, :], k_ref[:hi, :]) * att_scale
        rows = lax.broadcasted_iota(jnp.int32, (block, hi), 0) + lo
        cols = lax.broadcasted_iota(jnp.int32, (block, hi), 1)
        scores = jnp.where(rows >= cols, scores, -jnp.inf)
        peak = jnp.max(scores, axis=1, keepdims=True)
        exp_scores = jnp.exp(scores - peak)
        inverse = 1.0 / jnp.sum(exp_scores, axis=1, keepdims=True)
        probs_ref[0, 0, lo:hi, :hi] = exp_scores * inverse
        if hi < length:
            probs_ref[0, 0, lo:hi, hi:] = jnp.zeros((block, length - hi), jnp.float32)


def attention_probs(query_rows, key_rows):
    length = query_rows.shape[0] // SEQS
    heads = query_rows.shape[1] // HD
    tile = pl.BlockSpec((length, HD), lambda s, h: (s, h))
    return pl.pallas_call(
        probs_kernel,
        grid=(SEQS, heads),
        in_specs=[tile, tile],
        out_specs=pl.BlockSpec((1, 1, length, length), lambda s, h: (s, h, 0, 0)),
        out_shape=jax.ShapeDtypeStruct((SEQS, heads, length, length), jnp.float32),
        compiler_params=pltpu.CompilerParams(
            dimension_semantics=("arbitrary", "arbitrary"),
            vmem_limit_bytes=32 * 1024 * 1024,
        ),
        cost_estimate=pl.CostEstimate(
            flops=2 * SEQS * heads * length * length * HD,
            bytes_accessed=4 * SEQS * heads * length * (length + HD),
            transcendentals=SEQS * heads * length * length,
        ),
    )(query_rows, key_rows)


def attention_kernel(
    rows_ref, proj_ref, q_ref, k_ref, v_ref, probs_ref, gq_ref, gk_ref, gv_ref
):
    length = q_ref.shape[0]
    att_scale = HD ** (-0.5)
    block = row_block(length)
    count = length // block
    grad_part = dot_rt(rows_ref[...], proj_ref[...]).astype(jnp.bfloat16)
    grad_k = [None] * count
    grad_v = [None] * count
    for i in range(count):
        lo, hi = i * block, (i + 1) * block
        query = q_ref[lo:hi, :]
        grad_i = grad_part[lo:hi, :]
        probs = probs_ref[0, 0, lo:hi, :hi]
        probs_half = probs.astype(jnp.bfloat16)
        grad_probs = dot_rt(grad_i, v_ref[:hi, :])
        delta = jnp.sum(probs * grad_probs, axis=1, keepdims=True)
        grad_scores = (probs * (grad_probs - delta)).astype(jnp.bfloat16)
        gq_ref[lo:hi, :] = (
            att_scale * jnp.dot(grad_scores, k_ref[:hi, :], preferred_element_type=jnp.float32)
        ).astype(jnp.bfloat16)
        part_v = dot_lt(probs_half, grad_i)
        part_k = dot_lt(grad_scores, query)
        for j in range(i + 1):
            piece_v = part_v[j * block : (j + 1) * block, :]
            piece_k = part_k[j * block : (j + 1) * block, :]
            grad_v[j] = piece_v if grad_v[j] is None else grad_v[j] + piece_v
            grad_k[j] = piece_k if grad_k[j] is None else grad_k[j] + piece_k
    for j in range(count):
        gk_ref[j * block : (j + 1) * block, :] = (att_scale * grad_k[j]).astype(jnp.bfloat16)
        gv_ref[j * block : (j + 1) * block, :] = grad_v[j].astype(jnp.bfloat16)


def attention_grads(rows, proj, query_rows, key_rows, value_rows, probs):
    total, width = rows.shape
    length = total // SEQS
    heads = proj.shape[0] // HD
    tile = pl.BlockSpec((length, HD), lambda s, h: (s, h))
    out = jax.ShapeDtypeStruct(query_rows.shape, jnp.bfloat16)
    return pl.pallas_call(
        attention_kernel,
        grid=(SEQS, heads),
        in_specs=[
            pl.BlockSpec((length, width), lambda s, h: (s, 0)),
            pl.BlockSpec((HD, width), lambda s, h: (h, 0)),
            tile,
            tile,
            tile,
            pl.BlockSpec((1, 1, length, length), lambda s, h: (s, h, 0, 0)),
        ],
        out_specs=[tile, tile, tile],
        out_shape=[out, out, out],
        compiler_params=pltpu.CompilerParams(
            dimension_semantics=("arbitrary", "arbitrary"),
            vmem_limit_bytes=48 * 1024 * 1024,
        ),
    )(rows, proj, query_rows, key_rows, value_rows, probs)


def local(
    grad_out,
    hidden_in,
    norm_gain,
    expert_ids,
    gate_weights,
    gate_proj,
    up_proj,
    down_proj,
    out_proj,
    query_rows,
    key_rows,
    value_rows,
):
    tok_dev, model_width = grad_out.shape
    top_count = expert_ids.shape[1]
    groups = lax.axis_size("group")
    inner_size = lax.axis_size("inner")
    experts = groups * inner_size
    capacity = max(2, 5 * tok_dev * top_count // (4 * experts))
    near = 2
    far = inner_size // near
    plane = groups * near
    my_group = lax.axis_index("group")
    my_inner = lax.axis_index("inner")
    my_far = my_inner // near
    my_spot = my_group * near + my_inner % near

    def along(shift):
        pairs = []
        for dev in range(experts):
            g, i = divmod(dev, inner_size)
            f, n = divmod(i, near)
            pairs.append((dev, g * inner_size + (f ^ shift) * near + n))
        return pairs

    def across(turn):
        pairs = []
        for dev in range(experts):
            g, i = divmod(dev, inner_size)
            f, n = divmod(i, near)
            g2, n2 = divmod((g * near + n) ^ turn, near)
            pairs.append((dev, g2 * inner_size + f * near + n2))
        return pairs

    hid_full = hidden_in.astype(jnp.float32)
    inv_rms = lax.rsqrt(jnp.mean(hid_full * hid_full, axis=1, keepdims=True) + 1e-06)
    normal_rows = hid_full * inv_rms
    normed = (normal_rows * norm_gain).astype(jnp.bfloat16)
    token_rows = jnp.concatenate([grad_out, normed], axis=1)

    spots = my_spot ^ jnp.arange(plane, dtype=jnp.int32)
    plane_experts = (spots // near) * inner_size + my_far * near + spots % near
    before = (
        jnp.arange(tok_dev)[:, None] > jnp.arange(tok_dev)[None, :]
    ).astype(jnp.bfloat16)
    slots = jnp.arange(capacity, dtype=jnp.float32)

    chunk_rows = [token_rows]
    chunk_ids = [expert_ids]
    chunk_gates = [gate_weights]
    for s in range(1, far):
        chunk_ids.append(lax.ppermute(expert_ids, AXES, along(s)))
        chunk_gates.append(lax.ppermute(gate_weights, AXES, along(s)))
        chunk_rows.append(lax.ppermute(token_rows, AXES, along(s)))

    probs = attention_probs(query_rows, key_rows)

    total = None
    spare = 128
    for s in range(far):
        ids, gates, rows = chunk_ids[s], chunk_gates[s], chunk_rows[s]
        hit = ids[:, :, None] == plane_experts[None, None, :]
        match = jnp.any(hit, axis=1)
        gate_of = jnp.sum(jnp.where(hit, gates[:, :, None], 0.0), axis=1)
        rank = jnp.dot(before, match.astype(jnp.bfloat16), preferred_element_type=jnp.float32)
        place = jnp.where(match, rank, -1.0)
        put = (place.T[:, None, :] == slots[None, :, None]).astype(jnp.bfloat16)
        packed = jnp.dot(
            put.reshape(plane * capacity, tok_dev), rows, preferred_element_type=jnp.float32
        ).astype(jnp.bfloat16)
        packed = packed.reshape(plane, capacity, 2 * model_width)
        arrived = [packed[0]]
        for d in range(1, plane):
            arrived.append(lax.ppermute(packed[d], AXES, across(d)))
        arrived = jnp.concatenate(arrived, axis=0)
        pair_grad, gate_score = expert_backward(
            arrived[:, :model_width],
            arrived[:, model_width:],
            gate_proj[0],
            up_proj[0],
            down_proj[0],
        )
        tail = jnp.broadcast_to(gate_score[:, None], (plane * capacity, spare))
        pair_grad = jnp.concatenate([pair_grad, tail], axis=1)
        pair_grad = pair_grad.reshape(plane, capacity, model_width + spare)
        back = [pair_grad[0]]
        for d in range(1, plane):
            back.append(lax.ppermute(pair_grad[d], AXES, across(d)))
        back = jnp.concatenate(back, axis=0)
        score = back[:, model_width].astype(jnp.float32).reshape(plane, capacity)
        back = back[:, :model_width]
        picked = jnp.sum(
            jnp.where(place[:, :, None] == slots[None, None, :], score[None], 0.0), axis=2
        )
        gate_part = jnp.sum(jnp.where(hit, picked[:, None, :], 0.0), axis=2)
        weight = jnp.where(
            place[:, :, None] == slots[None, None, :], gate_of[:, :, None], 0.0
        ).reshape(tok_dev, plane * capacity)
        high = weight.astype(jnp.bfloat16)
        low = (weight - high.astype(jnp.float32)).astype(jnp.bfloat16)
        part = jnp.dot(high, back, preferred_element_type=jnp.float32) + jnp.dot(
            low, back, preferred_element_type=jnp.float32
        )
        part = jnp.concatenate(
            [part, jnp.pad(gate_part, ((0, 0), (0, spare - top_count)))], axis=1
        )
        if s > 0:
            part = part.astype(jnp.bfloat16)
            part = lax.ppermute(part, AXES, along(s))
            part = part.astype(jnp.float32)
        total = part if total is None else total + part
    moe_grad = total[:, :model_width]
    grad_gate = total[:, model_width : model_width + top_count].astype(jnp.bfloat16)

    scaled = moe_grad * norm_gain
    inner_mean = jnp.mean(scaled * normal_rows, axis=1, keepdims=True)
    grad_hidden = (
        grad_out.astype(jnp.float32) + inv_rms * (scaled - normal_rows * inner_mean)
    ).astype(jnp.bfloat16)
    gathered = lax.all_gather(grad_hidden, "inner", axis=0, tiled=True)
    grad_q, grad_k, grad_v = attention_grads(
        gathered, out_proj, query_rows, key_rows, value_rows, probs
    )
    return (grad_hidden, grad_gate, grad_q, grad_k, grad_v)


def solution(mesh):
    in_specs = (
        P(("group", "inner"), None),
        P(("group", "inner"), None),
        P(),
        P(("group", "inner"), None),
        P(("group", "inner"), None),
        P(("group", "inner"), None, None),
        P(("group", "inner"), None, None),
        P(("group", "inner"), None, None),
        P("inner", None),
        P("group", "inner"),
        P("group", "inner"),
        P("group", "inner"),
    )
    out_specs = (
        P(("group", "inner"), None),
        P(("group", "inner"), None),
        P("group", "inner"),
        P("group", "inner"),
        P("group", "inner"),
    )

    return jax.shard_map(local, mesh=mesh, in_specs=in_specs, out_specs=out_specs, check_vma=False)
```
